256 devices in a mesh: dp: 32 (over z, y), section: 2 (over x_lo), tensor: 4 (over x_hi, core).
Axes of the slice: x: 4 (x_hi: 2, x_lo: 2; x = x_hi * 2 + x_lo), y: 4, z: 8, core: 2. Of those that a mesh axis runs over, the one named last changes fastest.
Arguments:
- x_in: bfloat16 [3, 3072, 1536], P(None, 'dp'), may hold values from -6 to 6
- norm_gain: float32 [2, 1536], P('section'), may hold values from 0.1 to 1.9
- w_in: bfloat16 [2, 3, 1536, 1536], P('section', None, 'dp', 'tensor'), may hold values from -0.15625 to 0.15625
- w_out: bfloat16 [2, 3, 1536, 1536], P('section', None, 'tensor', 'dp'), may hold values from -0.15625 to 0.15625
- expert_ids: int32 [2, 3, 3072, 2], P('section', None, 'dp'), may hold values from 0 to 2, all different within a row
- gate_weights: float32 [2, 3, 3072, 2], P('section', None, 'dp'), may hold values from 0.1 to 0.9
- out_grad: bfloat16 [3, 3072, 1536], P(None, 'dp'), may hold values from -0.3125 to 0.3125
Outputs:
- grad_w_out: float32 [2, 3, 1536, 1536], P('section', None, 'tensor', 'dp')
- grad_gates: float32 [2, 3, 3072, 2], P('section', None, 'dp')
The draws below stay inside these ranges and needn't reach their ends.
Inputs may be any that keep to these rules, and one draw needn't show every extreme that they name: `expert_ids`: the 2 entries of one token name different experts, and every expert is named.
All inputs are finite; a program needn't handle non-finite values.
Results may differ from the reference program's by a relative error of at most 0.019.
Values may be sent and summed in bfloat16 or wider, within the bound.
No kernel may reach another device: no remote copies, remote signals or barrier semaphores. Data moves between devices by JAX's collectives and lax.ppermute only.
A program may use at most 64 MiB of HBM per device.

```python
import jax
import jax.numpy as jnp
from jax import lax

D = 1536
FF = 1536
EXP = 3
TOPK = 2
MICRO = 3
ROWS = 96
LAYERS = 2
TOKENS = 3072
N_DP = 32
N_TENSOR = 4


def block_scale(rng, dims, split, least, largest):
    def one(dim, shards_of):
        heights = jax.random.uniform(jax.random.fold_in(jax.random.fold_in(rng, 6), dim), (shards_of,), jnp.float32, least / len(split), largest / len(split))
        return jnp.repeat(jnp.exp(heights), dims[dim] // shards_of).reshape((-1,) + (1,) * (len(dims) - dim - 1))

    level = one(*split[0])
    for cut in split[1:]:
        level = level * one(*cut)
    return level


def different_ones(rng, rows, count, top, lift):
    order = jax.random.permutation(jax.random.fold_in(rng, 1), count)
    boost = order
    for power in range(3):
        boost = boost * boost // count
    boost = boost * lift // count
    tickets = jax.random.randint(jax.random.fold_in(rng, 2), (rows, count), 0, 4096) + boost
    sure = jax.random.permutation(jax.random.fold_in(rng, 3), rows)[jnp.arange(count) % rows]
    tickets = jnp.where(jnp.arange(rows)[:, None] == sure[None, :], 1 << 14, tickets)
    priority = tickets * count + jnp.arange(count)
    return lax.top_k(priority.astype(jnp.int32), top)[1].astype(jnp.int32)


def noise(rng, dims, width, limit, pieces=(), kind=jnp.bfloat16):
    loudness = block_scale(rng, dims, pieces, -0.22, 0.18) if pieces else 1.0
    array = jax.random.normal(rng, dims, jnp.float32) * width * loudness
    return jnp.minimum(jnp.maximum(array, -limit), limit).astype(kind)


def setup_inputs(seed: int = 0) -> dict:
    key_of = jax.random.split(jax.random.key(seed), 8)
    x_in = noise(key_of[0], (MICRO, TOKENS, D), 1.0, 6.0, ((1, 32),))
    norm_gain = jnp.clip(1.0 + 0.18 * jax.random.normal(key_of[1], (LAYERS, D), jnp.float32), 0.1, 1.9)
    w_in = noise(key_of[2], (LAYERS, EXP, D, FF), D ** -0.5, 0.15625, ((0, 2), (2, 32), (3, 4)))
    w_out = noise(key_of[3], (LAYERS, EXP, FF, D), FF ** -0.5, 0.15625, ((0, 2), (2, 4), (3, 32)))
    expert_ids = different_ones(key_of[4], LAYERS * MICRO * TOKENS, EXP, TOPK, 5461).reshape((LAYERS, MICRO, TOKENS, TOPK))
    gate_weights = jnp.clip(0.1 + 0.79999997 * jax.random.uniform(key_of[5], (LAYERS, MICRO, TOKENS, TOPK), jnp.float32) ** block_scale(key_of[5], (LAYERS, MICRO, TOKENS, TOPK), ((0, 2), (2, 32)), -0.2, 0.2), 0.1, 0.9)
    out_grad = noise(key_of[6], (MICRO, TOKENS, D), 0.05, 0.3125, ((1, 32),))
    return dict(x_in=x_in, norm_gain=norm_gain, w_in=w_in, w_out=w_out, expert_ids=expert_ids, gate_weights=gate_weights, out_grad=out_grad)


epsilon = 1e-05

def silu_slope(pre_act):
    sigmoid_value = jax.nn.sigmoid(pre_act)
    return sigmoid_value * (1.0 + pre_act * (1.0 - sigmoid_value))

def row_scale(values):
    widened = values.astype(jnp.float32)
    return (widened, lax.rsqrt(lax.optimization_barrier(jnp.mean(widened * widened, axis=-1, keepdims=True)) + epsilon))

def rounded(values):
    return lax.optimization_barrier(values.astype(jnp.bfloat16)).astype(jnp.float32)

def reference(x_in, norm_gain, w_in, w_out, expert_ids, gate_weights, out_grad):
    highest = lax.Precision.HIGHEST
    group_width = FF // N_TENSOR
    labels = jnp.arange(EXP, dtype=jnp.int32)
    routing = (expert_ids[..., None] == labels).astype(jnp.float32)
    gates_all = lax.optimization_barrier(jnp.sum(gate_weights[..., None] * routing, axis=3))
    inputs = [x_in[micro_index] for micro_index in range(MICRO)]
    saved = []
    for layer_index in range(LAYERS):
        saved.append(list(inputs))
        w_in_wide = w_in[layer_index].astype(jnp.float32)
        w_out_wide = w_out[layer_index].astype(jnp.float32)
        outputs = []
        for micro_index in range(MICRO):
            layer_input = inputs[micro_index]
            widened, inv_rms = row_scale(layer_input)
            normed = rounded(widened * inv_rms * norm_gain[layer_index])
            gate_rows = gates_all[layer_index, micro_index].T[:, :, None]
            summed = widened
            for group_index in range(N_TENSOR):
                low = group_index * group_width
                pre_act = jnp.einsum('td,edf->etf', normed, w_in_wide[:, :, low:low + group_width], precision=highest)
                hidden = rounded(gate_rows * jax.nn.silu(pre_act))
                partial_out = jnp.einsum('etf,efd->td', hidden, w_out_wide[:, low:low + group_width, :], precision=highest)
                summed = summed + rounded(partial_out)
            outputs.append(summed.astype(jnp.bfloat16))
        inputs = outputs
    grads = [out_grad[micro_index] for micro_index in range(MICRO)]
    weight_grads = []
    gate_grad_layers = []
    for layer_index in reversed(range(LAYERS)):
        w_in_wide = w_in[layer_index].astype(jnp.float32)
        w_out_wide = w_out[layer_index].astype(jnp.float32)
        accumulated = jnp.zeros((EXP, N_DP, FF, D), jnp.float32)
        new_grads = []
        gate_grad_micro = []
        for micro_index in range(MICRO):
            grad_wide = grads[micro_index].astype(jnp.float32)
            widened, inv_rms = row_scale(saved[layer_index][micro_index])
            normed = rounded(widened * inv_rms * norm_gain[layer_index])
            gate_rows = gates_all[layer_index, micro_index].T[:, :, None]
            grad_normed = jnp.zeros((TOKENS, D), jnp.float32)
            gate_total = jnp.zeros((TOKENS, EXP), jnp.float32)
            hidden_groups = []
            for group_index in range(N_TENSOR):
                low = group_index * group_width
                pre_act = jnp.einsum('td,edf->etf', normed, w_in_wide[:, :, low:low + group_width], precision=highest)
                activated = jax.nn.silu(pre_act)
                grad_hidden = jnp.einsum('td,efd->etf', grad_wide, w_out_wide[:, low:low + group_width, :], precision=highest)
                gate_total = gate_total + rounded(lax.optimization_barrier(jnp.sum(activated * grad_hidden, axis=2)).T)
                hidden_groups.append(rounded(gate_rows * activated))
                grad_pre = rounded(gate_rows * grad_hidden * silu_slope(pre_act))
                grad_normed = grad_normed + rounded(jnp.einsum('etf,edf->td', grad_pre, w_in_wide[:, :, low:low + group_width], precision=highest))
            hidden_all = jnp.concatenate(hidden_groups, axis=2)
            accumulated = accumulated + jnp.einsum('eirf,ird->eifd', hidden_all.reshape(EXP, N_DP, ROWS, FF), grad_wide.reshape(N_DP, ROWS, D), precision=highest)
            scaled_grad = grad_normed * norm_gain[layer_index]
            projection = lax.optimization_barrier(jnp.mean(scaled_grad * widened, axis=-1, keepdims=True))
            new_grads.append((grad_wide + inv_rms * (scaled_grad - widened * inv_rms * inv_rms * projection)).astype(jnp.bfloat16))
            gate_grad_micro.append(lax.optimization_barrier(jnp.sum(gate_total[:, None, :] * routing[layer_index, micro_index], axis=2)))
        weight_grads.insert(0, lax.optimization_barrier(jnp.sum(rounded(accumulated), axis=1)))
        gate_grad_layers.insert(0, jnp.stack(gate_grad_micro))
        grads = new_grads
    return (jnp.stack(weight_grads), jnp.stack(gate_grad_layers))
```

```python
import jax
import jax.numpy as jnp
from jax import lax
from jax.sharding import PartitionSpec as P

epsilon = 1e-05


def silu_slope(pre_act):
    sigmoid_value = jax.nn.sigmoid(pre_act)
    return sigmoid_value * (1.0 + pre_act * (1.0 - sigmoid_value))


def inverse_rms(widened):
    return lax.rsqrt(jnp.mean(widened * widened, axis=-1, keepdims=True) + epsilon)


def swap_cores(shard):
    length = lax.axis_size("tensor")
    return lax.ppermute(shard, "tensor", [(i, i ^ 1) for i in range(length)])


def to_section(shard, source, target):
    length = lax.axis_size("tensor")
    near, far = [
        lax.ppermute(
            shard,
            ("section", "tensor"),
            [(source * length + i, target * length + (i ^ flip)) for i in range(length)],
        )
        for flip in (0, 2)
    ]
    return near.astype(jnp.float32) + far.astype(jnp.float32)


def sum_over_cores(partial):
    half = partial.shape[0] // 2
    other = swap_cores(partial[half:])
    return partial[:half].astype(jnp.float32) + other.astype(jnp.float32)


def whole_rows(half):
    return jnp.concatenate([half, swap_cores(half)], axis=0)


def local_order(array, core):
    half = array.shape[0] // 2
    return jnp.where(core == 0, array, jnp.roll(array, half, axis=0))


def local(x_in, norm_gain, w_in, w_out, expert_ids, gate_weights, out_grad):
    position = lax.axis_index("section")
    core = lax.axis_index("tensor") % 2
    micro_count, row_count, feature_count = x_in.shape
    rows = micro_count * row_count
    half = rows // 2
    _, experts, owned, hidden_cols = w_in.shape
    wide = experts * hidden_cols
    gain = norm_gain[0]

    stacked = jnp.concatenate(
        [
            w_in[0].transpose(1, 0, 2).reshape(owned, wide),
            w_out[0].transpose(2, 0, 1).reshape(owned, wide),
        ],
        axis=1,
    )
    gathered = lax.all_gather(stacked, "dp", axis=0, tiled=True)
    w_in_full = gathered[:, :wide]
    w_out_full = gathered[:, wide:]

    labels = jnp.arange(experts, dtype=jnp.int32)
    routing = (expert_ids[0].reshape(rows, -1)[..., None] == labels).astype(jnp.float32)
    gates = jnp.sum(gate_weights[0].reshape(rows, -1)[..., None] * routing, axis=1)
    gates = local_order(gates, core)
    x_first = local_order(x_in.reshape(rows, feature_count), core)
    grad_last = local_order(out_grad.reshape(rows, feature_count), core)

    def spread(gate_rows):
        return jnp.repeat(gate_rows, hidden_cols, axis=1)

    def project_in(layer_input):
        widened = layer_input.astype(jnp.float32)
        normed = (widened * inverse_rms(widened) * gain).astype(jnp.bfloat16)
        return jnp.einsum("td,dk->tk", normed, w_in_full, preferred_element_type=jnp.float32)

    def hidden_of(pre_act):
        return (spread(gates) * jax.nn.silu(pre_act)).astype(jnp.bfloat16)

    def grad_hidden_of(grad_now):
        return jnp.einsum("td,dk->tk", grad_now, w_out_full, preferred_element_type=jnp.float32)

    def gate_part_of(pre_act, grad_hidden):
        product = jax.nn.silu(pre_act) * grad_hidden
        return jnp.sum(product.reshape(rows, experts, hidden_cols), axis=2).astype(jnp.bfloat16)

    pre_first = project_in(x_first)
    hidden_first = hidden_of(pre_first)
    part = jnp.einsum(
        "tk,dk->td", hidden_first, w_out_full, preferred_element_type=jnp.float32
    ).astype(jnp.bfloat16)
    arrived = to_section(sum_over_cores(part).astype(jnp.bfloat16), 0, 1)
    x_half = (x_first[:half].astype(jnp.float32) + arrived).astype(jnp.bfloat16)
    x_second = whole_rows(x_half)

    grad_hidden_second = grad_hidden_of(grad_last)
    pre_second = project_in(x_second)
    grad_pre = (spread(gates) * grad_hidden_second * silu_slope(pre_second)).astype(jnp.bfloat16)
    grad_part = jnp.einsum(
        "tk,dk->td", grad_pre, w_in_full, preferred_element_type=jnp.float32
    ).astype(jnp.bfloat16)
    scaled = sum_over_cores(grad_part) * gain
    widened = x_half.astype(jnp.float32)
    inv_rms = inverse_rms(widened)
    projection = jnp.mean(scaled * widened, axis=-1, keepdims=True)
    change = inv_rms * (scaled - widened * inv_rms * inv_rms * projection)
    arrived = to_section(change.astype(jnp.bfloat16), 1, 0)
    grad_half = (grad_last[:half].astype(jnp.float32) + arrived).astype(jnp.bfloat16)
    grad_first = whole_rows(grad_half)

    grad_hidden_first = grad_hidden_of(grad_first)
    is_first = position == 0
    gate_part = jnp.where(
        is_first,
        gate_part_of(pre_first, grad_hidden_first),
        gate_part_of(pre_second, grad_hidden_second),
    )
    length = lax.axis_size("tensor")
    gate_total = gate_part.astype(jnp.float32)
    for flip in range(1, length):
        mate = lax.ppermute(gate_part, "tensor", [(i, i ^ flip) for i in range(length)])
        if flip % 2:
            mate = jnp.roll(mate, half, axis=0)
        gate_total = gate_total + mate.astype(jnp.float32)
    gate_total = local_order(gate_total, core)
    grad_gates = jnp.sum(gate_total[:, None, :] * routing, axis=2)

    hidden_own = jnp.where(is_first, hidden_first, hidden_of(pre_second))
    grad_own = jnp.where(is_first, grad_first, grad_last)
    pieces = jnp.einsum(
        "td,tk->dk", grad_own, hidden_own, preferred_element_type=jnp.float32
    ).astype(jnp.bfloat16)
    groups = lax.axis_size("dp")
    exchanged = lax.all_to_all(pieces.reshape(groups, owned, wide), "dp", 0, 0, tiled=True)
    total = jnp.sum(exchanged.astype(jnp.float32), axis=0)
    grad_w_out = total.reshape(owned, experts, hidden_cols).transpose(1, 2, 0)
    return (grad_w_out[None], grad_gates.reshape((1, micro_count, row_count, -1)))


def solution(mesh):
    placed = (
        P(None, "dp", None),
        P("section", None),
        P("section", None, "dp", "tensor"),
        P("section", None, "tensor", "dp"),
        P("section", None, "dp", None),
        P("section", None, "dp", None),
        P(None, "dp", None),
    )
    return jax.shard_map(
        local,
        mesh=mesh,
        in_specs=placed,
        out_specs=(P("section", None, "tensor", "dp"), P("section", None, "dp", None)),
        check_vma=False,
    )
```

```python
import jax
import jax.numpy as jnp
from jax import lax
from jax.sharding import PartitionSpec as P

epsilon = 1e-05
inner_size = 4


def take_from(shard, by_outer, by_inner):
    length = lax.axis_size("dp")
    outer = length // inner_size
    pairs = []
    for z in range(outer):
        for y in range(inner_size):
            source = ((z + by_outer) % outer) * inner_size + (y + by_inner) % inner_size
            pairs.append((source, z * inner_size + y))
    return lax.ppermute(shard, "dp", pairs)


def along_z(shard, step):
    return take_from(shard, step, 0)


def along_y(shard, step):
    return take_from(shard, 0, step)


def rows_of(shard):
    experts, rows, columns = shard.shape
    return shard.transpose(1, 0, 2).reshape(rows, experts * columns)


def slot(step, outer):
    return (step + 2) % outer


def gather_weights(z_first, y_first, later):
    outer = lax.axis_size("dp") // inner_size
    steps = (1, -1, 2, -2)
    near = [along_z(z_first, step) for step in steps]
    beside = [along_y(y_first, step) for step in (1, 2, -1)]
    near, beside, later = lax.optimization_barrier((near, beside, later))
    at_z = dict(zip(steps, near))
    at_z[0] = z_first
    owned = z_first.shape[1]

    block = jnp.concatenate([rows_of(part) for part in [y_first] + beside])
    blocks = {0: block}
    up = down = block
    for step in range(1, outer // 2):
        up, down = along_z(up, 1), along_z(down, -1)
        blocks[step], blocks[outer - step] = up, down
        if step == 1:
            at_z[3], at_z[-3] = along_z(at_z[2], 1), along_z(at_z[-2], -1)
            at_z[4] = along_z(at_z[2], 2)
            first = jnp.concatenate([rows_of(at_z[k]) for k in (-2, -1, 0, 1, 2)])
            wide = first.shape[1]
            first_up, first_down = along_y(first, 1), along_y(first, -1)
            second = jnp.concatenate([rows_of(at_z[k]) for k in (3, 4, -3)])
            second_up, second_down = along_y(second, 1), along_y(second, -1)
            first_far, second_far = along_y(first_up, 1), along_y(second_down, -1)
    middle = block.shape[0] // 2
    blocks[outer // 2] = jnp.concatenate([along_z(up[:middle], 1), along_z(down[middle:], -1)])
    order = sorted(range(outer), key=lambda step: slot(step, outer))
    y_first_whole = jnp.concatenate([blocks[step] for step in order])

    def interleaved(*columns):
        return jnp.concatenate([c.reshape(-1, 1, owned, wide) for c in columns], axis=1)

    z_first_whole = jnp.concatenate(
        [
            interleaved(first, first_up, first_far, first_down),
            interleaved(second, second_up, second_far, second_down),
        ]
    ).reshape(-1, wide)
    return z_first_whole, y_first_whole, later


def wide_sum(*terms):
    total = terms[0].astype(jnp.float32)
    for term in terms[1:]:
        total = total + term.astype(jnp.float32)
    return total


def ring_reduce(blocks, size, shift):
    opposite = blocks[size // 2]
    middle = opposite.shape[0] // 2
    arrived = []
    for sign, sent, rest in (
        (1, opposite[:middle], slice(None, middle)),
        (-1, opposite[middle:], slice(middle, None)),
    ):
        moving = shift(sent, -sign)
        for step in range(size // 2 - 1, 0, -1):
            mine = blocks[(sign * step) % size]
            if step == size // 2 - 1:
                low = mine[:middle] if sign > 0 else mine[middle:]
                added = wide_sum(low, moving).astype(mine.dtype)
                pieces = [added, mine[middle:]] if sign > 0 else [mine[:middle], added]
                summed = jnp.concatenate(pieces)
            else:
                summed = wide_sum(mine, moving).astype(mine.dtype)
            moving = shift(summed, -sign)
        arrived.append(moving)
    return wide_sum(blocks[0], *arrived)


def direct_reduce(blocks, size, shift):
    return wide_sum(blocks[0], *[shift(blocks[step], -step) for step in range(1, size)])


def scatter_outer_first(pieces):
    outer = pieces.shape[0]
    blocks = [pieces[slot(k, outer)] for k in range(outer)]
    mine = ring_reduce(blocks, outer, along_z).astype(pieces.dtype)
    return direct_reduce([mine[k] for k in range(inner_size)], inner_size, along_y)


def scatter_inner_first(pieces):
    outer = pieces.shape[0]
    mine = ring_reduce([pieces[:, k] for k in range(inner_size)], inner_size, along_y)
    mine = mine.astype(pieces.dtype)
    return direct_reduce([mine[slot(k, outer)] for k in range(outer)], outer, along_z)


def silu_slope(pre_act):
    sigmoid_value = jax.nn.sigmoid(pre_act)
    return sigmoid_value * (1.0 + pre_act * (1.0 - sigmoid_value))


def inverse_rms(widened):
    return lax.rsqrt(jnp.mean(widened * widened, axis=-1, keepdims=True) + epsilon)


def swap_cores(shard):
    length = lax.axis_size("tensor")
    return lax.ppermute(shard, "tensor", [(i, i ^ 1) for i in range(length)])


def to_section(shard, source, target):
    length = lax.axis_size("tensor")
    near, far = [
        lax.ppermute(
            shard,
            ("section", "tensor"),
            [(source * length + i, target * length + (i ^ flip)) for i in range(length)],
        )
        for flip in (0, 2)
    ]
    return near.astype(jnp.float32) + far.astype(jnp.float32)


def sum_over_cores(partial):
    half = partial.shape[0] // 2
    other = swap_cores(partial[half:])
    return partial[:half].astype(jnp.float32) + other.astype(jnp.float32)


def whole_rows(half):
    return jnp.concatenate([half, swap_cores(half)], axis=0)


def local_order(array, core):
    half = array.shape[0] // 2
    return jnp.where(core == 0, array, jnp.roll(array, half, axis=0))


def local(x_in, norm_gain, w_in, w_out, expert_ids, gate_weights, out_grad):
    position = lax.axis_index("section")
    core = lax.axis_index("tensor") % 2
    micro_count, row_count, feature_count = x_in.shape
    rows = micro_count * row_count
    half = rows // 2
    _, experts, owned, hidden_cols = w_in.shape
    wide = experts * hidden_cols

    tokens = (x_in, out_grad, expert_ids, gate_weights, norm_gain)
    w_in_full, w_out_full, tokens = gather_weights(w_in[0], w_out[0].transpose(0, 2, 1), tokens)
    x_in, out_grad, expert_ids, gate_weights, norm_gain = tokens

    labels = jnp.arange(experts, dtype=jnp.int32)
    routing = (expert_ids[0].reshape(rows, -1)[..., None] == labels).astype(jnp.float32)
    gates = jnp.sum(gate_weights[0].reshape(rows, -1)[..., None] * routing, axis=1)
    gates = local_order(gates, core)

    groups = lax.axis_size("dp")
    outer = groups // inner_size
    here_z, here_y = jnp.divmod(lax.axis_index("dp"), inner_size)
    feature = jnp.arange(feature_count, dtype=jnp.int32)
    block_z, block_y = feature // (inner_size * owned), feature // owned % inner_size
    there = (block_z + here_z + outer - slot(0, outer)) % outer * inner_size
    there = (there + (block_y + here_y) % inner_size) * owned + feature % owned
    moved = feature[:, None] == there[None, :]
    both = jnp.concatenate(
        [
            local_order(x_in.reshape(rows, feature_count), core),
            local_order(out_grad.reshape(rows, feature_count), core),
        ]
    )
    both = jnp.einsum(
        "td,dc->tc", both, moved.astype(jnp.bfloat16), preferred_element_type=jnp.float32
    ).astype(jnp.bfloat16)
    x_first, grad_last = both[:rows], both[rows:]
    gain = jnp.sum(jnp.where(moved, norm_gain[0][:, None], 0.0), axis=0)

    def spread(gate_rows):
        return jnp.repeat(gate_rows, hidden_cols, axis=1)

    def project_in(layer_input):
        widened = layer_input.astype(jnp.float32)
        normed = (widened * inverse_rms(widened) * gain).astype(jnp.bfloat16)
        return jnp.einsum("td,dk->tk", normed, w_in_full, preferred_element_type=jnp.float32)

    def hidden_of(pre_act):
        return (spread(gates) * jax.nn.silu(pre_act)).astype(jnp.bfloat16)

    def grad_hidden_of(grad_now):
        return jnp.einsum("td,dk->tk", grad_now, w_out_full, preferred_element_type=jnp.float32)

    def gate_part_of(pre_act, grad_hidden):
        product = jax.nn.silu(pre_act) * grad_hidden
        return jnp.sum(product.reshape(rows, experts, hidden_cols), axis=2).astype(jnp.bfloat16)

    pre_first = project_in(x_first)
    hidden_first = hidden_of(pre_first)
    part = jnp.einsum(
        "tk,dk->td", hidden_first, w_out_full, preferred_element_type=jnp.float32
    ).astype(jnp.bfloat16)
    arrived = to_section(sum_over_cores(part).astype(jnp.bfloat16), 0, 1)
    x_half = (x_first[:half].astype(jnp.float32) + arrived).astype(jnp.bfloat16)
    x_second = whole_rows(x_half)

    grad_hidden_second = grad_hidden_of(grad_last)
    pre_second = project_in(x_second)
    grad_pre = (spread(gates) * grad_hidden_second * silu_slope(pre_second)).astype(jnp.bfloat16)
    grad_part = jnp.einsum(
        "tk,dk->td", grad_pre, w_in_full, preferred_element_type=jnp.float32
    ).astype(jnp.bfloat16)
    scaled = sum_over_cores(grad_part) * gain
    widened = x_half.astype(jnp.float32)
    inv_rms = inverse_rms(widened)
    projection = jnp.mean(scaled * widened, axis=-1, keepdims=True)
    change = inv_rms * (scaled - widened * inv_rms * inv_rms * projection)
    change = change.astype(jnp.bfloat16)
    arrived = to_section(change, 1, 0)
    gate_part_second = gate_part_of(pre_second, grad_hidden_second)
    arrived, gate_part_second = lax.optimization_barrier((arrived, gate_part_second))
    grad_half = (grad_last[:half].astype(jnp.float32) + arrived).astype(jnp.bfloat16)
    grad_first = whole_rows(grad_half)

    is_first = position == 0
    hidden_own = jnp.where(is_first, hidden_first, hidden_of(pre_second))
    grad_own = jnp.where(is_first, grad_first, grad_last)
    pieces = jnp.einsum(
        "td,tk->dk", grad_own, hidden_own, preferred_element_type=jnp.float32
    ).astype(jnp.bfloat16)
    pieces = pieces.reshape(outer, inner_size, owned, wide)
    pieces, grad_first = lax.optimization_barrier((pieces, grad_first))
    split = wide // 2 // 128 * 128
    total = jnp.concatenate(
        [scatter_inner_first(pieces[..., :split]), scatter_outer_first(pieces[..., split:])], axis=1
    )
    grad_w_out = total.reshape(owned, experts, hidden_cols).transpose(1, 2, 0)

    gate_part_first = gate_part_of(pre_first, grad_hidden_of(grad_first))
    gate_part = jnp.where(is_first, gate_part_first, gate_part_second)
    length = lax.axis_size("tensor")
    gate_total = gate_part.astype(jnp.float32)
    for flip in range(1, length):
        mate = lax.ppermute(gate_part, "tensor", [(i, i ^ flip) for i in range(length)])
        if flip % 2:
            mate = jnp.roll(mate, half, axis=0)
        gate_total = gate_total + mate.astype(jnp.float32)
    gate_total = local_order(gate_total, core)
    grad_gates = jnp.sum(gate_total[:, None, :] * routing, axis=2)
    return (grad_w_out[None], grad_gates.reshape((1, micro_count, row_count, -1)))


def solution(mesh):
    placed = (
        P(None, "dp", None),
        P("section", None),
        P("section", None, "dp", "tensor"),
        P("section", None, "tensor", "dp"),
        P("section", None, "dp", None),
        P("section", None, "dp", None),
        P(None, "dp", None),
    )
    return jax.shard_map(
        local,
        mesh=mesh,
        in_specs=placed,
        out_specs=(P("section", None, "tensor", "dp"), P("section", None, "dp", None)),
        check_vma=False,
    )
```
